32 devices in a mesh: groups: 2 (over x), ctx: 16 (over z, y, core).
Axes of the slice: x: 2, y: 2, z: 4, core: 2. Of those that a mesh axis runs over, the one named last changes fastest.
Arguments:
- tokens: bfloat16 [3072, 1152], P(('groups', 'ctx')), parts along dimension 0, may hold values from -100 to 100
- owner: int32 [3072, 1], P(('groups', 'ctx')), parts along dimension 0, may hold values from 0 to 15; in each aligned block of 96 rows (0 to 95, 96 to 191, ...) at most 12 rows name the same one
- slot_map: int32 [32, 16, 12], P(('groups', 'ctx')), parts along dimension 0, may hold values from 0 to 47
- sizes: int32 [3072], P(('groups', 'ctx')), parts along dimension 0, may hold values from 1 to 4
- w_query: bfloat16 [1152, 576], replicated, may hold values from -0.1875 to 0.1875
- w_key: bfloat16 [1152, 576], replicated, may hold values from -0.1875 to 0.1875
- w_value: bfloat16 [1152, 576], replicated, may hold values from -0.1875 to 0.1875
- w_out: bfloat16 [576, 1152], replicated, may hold values from -0.25 to 0.25
Outputs:
- mixed: bfloat16 [3072, 1152], P(('groups', 'ctx')), parts along dimension 0
The draws below stay inside these ranges and needn't reach their ends.
There are 2 independent parts, one for each index of `groups`. The reference program is written for one: setup_inputs(seed, part) draws one part's arguments, and reference() takes and returns one part's arrays. A program takes and returns all parts, laid end to end along the dimension named above; an argument that names none is the same for every part. Nothing has to cross between parts.
Inputs may be any that keep to these rules, and one draw needn't show every extreme that they name: Among the source tokens of one index of ctx, at most 12 name the same owner, and in some index exactly 12 do.
All inputs are finite; a program needn't handle non-finite values.
Results may differ from the reference program's by a relative error of at most 0.0085.
The reference program's roundings to bfloat16 on the way (of `merged`, `key_bias`, `attended` and `merged_out`) count: a program that leaves them out, or rounds other values in their place, can miss the bound.
Values may be sent and summed in bfloat16 or wider, within the bound.
A program may use at most 128 MiB of HBM per device.

```python
import math
import jax
import jax.numpy as jnp
import numpy as np
from jax import lax

D = 1152
HEADS = 8
HEAD = 72
TOK_DEV = 96
MDEV = 48
SHARDS = 16
SLOT = 12
TOKENS = 1536
MTOT = 768


def draw_tokens(key, part):
    base = jax.random.normal(key, (TOKENS, D), jnp.float32)
    base = jnp.clip(base, -6.0, 6.0)
    return base.astype(jnp.bfloat16)


def set_ends(values, rng, low, largest):
    longest = values.shape.index(max(values.shape))
    spots = []
    for shift in (0, 1):
        where = [jax.random.randint(jax.random.fold_in(rng, axis), (), 0, length) for axis, length in enumerate(values.shape)]
        where[longest] = (where[longest] + shift) % values.shape[longest]
        spots.append(tuple(where))
    return values.at[spots[0]].set(low).at[spots[1]].set(largest)


def assign_block(stream_key, own, number, rows, number_of, top, bound, lean):
    order = jax.random.permutation(stream_key, number_of)
    packed, ordinary = shares(number_of, rows * top, bound, lean, True), shares(number_of, rows * top, bound, lean, False)
    places = jnp.arange(number_of)

    def named(tallies, rotation):
        used = int((tallies > 0).sum())
        fixed = max(1, used // 4)
        moved = fixed + (places - fixed + rotation * (used - fixed)) % max(1, number_of - fixed)
        return jnp.zeros((number_of,), jnp.int32).at[order[jnp.where(places < fixed, places, moved)]].set(jnp.asarray(tallies, jnp.int32))

    tallies = jnp.where(number % 4 == 0, named(packed, number // 4), named(ordinary, number - number // 4 - 1))
    mixed = jax.random.permutation(jax.random.fold_in(own, 3), number_of)
    donor, receiver = mixed[0:number_of // 2 * 2:2], mixed[1:number_of // 2 * 2:2]
    room = jnp.minimum(tallies[donor] - 1, bound - tallies[receiver]) // 2
    room = jnp.where((donor == order[0]) | (receiver == order[0]) | (tallies[receiver] == 0), 0, jnp.maximum(room, 0))
    moved = jax.random.randint(jax.random.fold_in(own, 4), (number_of // 2,), 0, 1 << 20) % (room + 1)
    tallies = tallies.at[donor].add(-moved).at[receiver].add(moved)
    labels = jnp.searchsorted(jnp.cumsum(tallies), jnp.arange(rows * top), side="right").astype(jnp.int32)
    grid = labels.reshape(top, rows).T
    grid = grid[jax.random.permutation(jax.random.fold_in(own, 1), rows)]
    rotation = jax.random.randint(jax.random.fold_in(own, 2), (rows, 1), 0, top)
    return jnp.take_along_axis(grid, (jnp.arange(top)[None, :] + rotation) % top, axis=1)


def shares(count, total, bound, slope, full):
    portions = [(1 << 20) // math.isqrt(standing ** slope) + 1 for standing in range(1, count + 1)]
    largest = bound if full else min(bound, max(-(-total // count), total * portions[0] // sum(portions)))
    least = 1 if total - largest >= count - 1 else 0
    given, surplus = [largest] + [least] * (count - 1), total - largest - least * (count - 1)
    while surplus > 0:
        candidates = [i for i in range(1, count) if given[i] < largest] or [i for i in range(1, count) if given[i] < bound]
        mass, budget = sum([portions[i] for i in candidates]), surplus
        for i in candidates:
            more = min(bound - given[i], max(1, budget * portions[i] // mass), surplus)
            given[i] = given[i] + more
            surplus = surplus - more
    return np.array(given)


def scatter_about(rng, dims, scale, most, held_as=jnp.bfloat16):
    values = jax.random.normal(rng, dims, jnp.float32) * scale
    return jnp.minimum(jnp.maximum(values, -most), most).astype(held_as)


def setup_inputs(seed: int = 0, part: int = 0) -> dict:
    seeds = jax.random.split(jax.random.key(seed), 9)
    part_splits = jax.random.split(jax.random.fold_in(seeds[8], part), 9)
    tokens = draw_tokens(jax.random.fold_in(jax.random.fold_in(seeds[8], part), 71), part)
    owner_keys = jax.random.split(jax.random.fold_in(part_splits[1], 1), TOKENS // TOK_DEV)
    owner_turns = jax.random.permutation(jax.random.fold_in(part_splits[1], 3), TOKENS // TOK_DEV)
    owner = jax.vmap(lambda own, number: assign_block(jax.random.fold_in(part_splits[1], 2), own, number, TOK_DEV, SHARDS, 1, SLOT, 2))(owner_keys, owner_turns).reshape((TOKENS, 1))
    slot_map = set_ends(jax.random.randint(part_splits[2], (SHARDS, SHARDS, SLOT), 0, MDEV), jax.random.fold_in(part_splits[2], 1), 0, MDEV - 1).astype(jnp.int32)
    sizes = set_ends(jax.random.randint(part_splits[3], (TOKENS,), 1, 5), jax.random.fold_in(part_splits[3], 1), 1, 4).astype(jnp.int32)
    w_query = scatter_about(seeds[4], (D, HEADS * HEAD), D ** -0.5, 0.1875)
    w_key = scatter_about(seeds[5], (D, HEADS * HEAD), D ** -0.5, 0.1875)
    w_value = scatter_about(seeds[6], (D, HEADS * HEAD), D ** -0.5, 0.1875)
    w_out = scatter_about(seeds[7], (HEADS * HEAD, D), (HEADS * HEAD) ** -0.5, 0.25)
    return dict(tokens=tokens, owner=owner, slot_map=slot_map, sizes=sizes, w_query=w_query, w_key=w_key, w_value=w_value, w_out=w_out)


def reference(tokens, owner, slot_map, sizes, w_query, w_key, w_value, w_out):
    owners = owner[:, 0].reshape(SHARDS, TOK_DEV).astype(jnp.int32)
    marks = (owners[:, :, None] == jnp.arange(SHARDS, dtype=jnp.int32)[None, None, :]).astype(jnp.int32)
    ranking = lax.optimization_barrier(jnp.sum((jnp.cumsum(marks, axis=1) - marks) * marks, axis=2)).astype(jnp.int32)
    senders = jnp.broadcast_to(jnp.arange(SHARDS, dtype=jnp.int32)[:, None], (SHARDS, TOK_DEV))
    dest = (owners * MDEV + slot_map[owners, senders, ranking]).reshape(TOKENS).astype(jnp.int32)
    weights = sizes.astype(jnp.float32)
    counts = jax.ops.segment_sum(weights, dest, num_segments=MTOT)
    merged_sum = jax.ops.segment_sum(weights[:, None] * tokens.astype(jnp.float32), dest, num_segments=MTOT)
    merged = (merged_sum / jnp.maximum(counts, 1.0)[:, None]).astype(jnp.bfloat16)
    bias_low = jnp.where(counts > 0, jnp.log(jnp.maximum(counts, 1.0)), -1e+30).astype(jnp.bfloat16)
    key_bias = lax.optimization_barrier(bias_low).astype(jnp.float32)
    queries = jnp.dot(merged, w_query, preferred_element_type=jnp.float32).astype(jnp.bfloat16)
    keys = jnp.dot(merged, w_key, preferred_element_type=jnp.float32).astype(jnp.bfloat16)
    values = jnp.dot(merged, w_value, preferred_element_type=jnp.float32).astype(jnp.bfloat16)
    key_heads = keys.reshape(MTOT, HEADS, HEAD).astype(jnp.float32)
    value_heads = values.reshape(MTOT, HEADS, HEAD).astype(jnp.float32)
    inverse = 1.0 / math.sqrt(HEAD)
    block = math.gcd(MTOT, 512)

    def block_attend(query_block):
        scores = jnp.einsum('qhd,khd->hqk', query_block.astype(jnp.float32), key_heads) * inverse
        scores = scores + key_bias[None, None, :]
        top = lax.optimization_barrier(jnp.max(scores, axis=2, keepdims=True))
        expo = jnp.exp(scores - top)
        total = lax.optimization_barrier(jnp.sum(expo, axis=2))
        rounded = lax.optimization_barrier(expo.astype(jnp.bfloat16)).astype(jnp.float32)
        accum = jnp.einsum('hqk,khd->hqd', rounded, value_heads)
        result = accum / total[:, :, None]
        return jnp.transpose(result, (1, 0, 2)).reshape(block, HEADS * HEAD).astype(jnp.bfloat16)
    attended = lax.map(block_attend, queries.reshape(MTOT // block, block, HEADS, HEAD))
    attended = attended.reshape(MTOT, HEADS * HEAD)
    merged_out = jnp.dot(attended, w_out, preferred_element_type=jnp.float32).astype(jnp.bfloat16)
    return merged_out[dest]
```

```python
import functools
import math

import jax
import jax.numpy as jnp
from jax import lax
from jax.experimental import pallas as pl
from jax.experimental.pallas import tpu as pltpu
from jax.sharding import PartitionSpec as P

HEADS = 8
HEAD = 72
LANES = 128
MESH = pl.DeviceIdType.MESH


def iota(shape, axis):
    return lax.broadcasted_iota(jnp.int32, shape, axis)


def kernel(
    shards,
    tok_ref,
    owner_ref,
    slot_ref,
    sizes_ref,
    wq_hbm,
    wk_hbm,
    wv_hbm,
    wo_hbm,
    out_ref,
    wq,
    wk,
    wv,
    wo,
    wo_pad,
    slots_in,
    outgoing,
    incoming,
    landed,
    dest_out,
    dest_in,
    heads_out,
    heads_in,
    att_out,
    att_in,
    w_sem,
    slot_send,
    slot_recv,
    tok_send,
    tok_recv,
    dest_send,
    dest_recv,
    head_send,
    head_recv,
    share_send,
    att_send,
    att_recv,
    own_sem,
):
    group = lax.axis_index("groups")
    me = lax.axis_index("ctx")
    reps = shards // HEADS
    my_head = me // reps
    my_rep = lax.rem(me, reps)
    tokens, width = tok_ref.shape
    slots = slot_ref.shape[2]
    padded = landed.shape[0] // shards
    places = landed.shape[0]
    merged_rows = heads_out.shape[1]
    total_rows = shards * merged_rows
    model = HEADS * HEAD
    pack = heads_out.shape[2]

    def remote(src, dst, send, recv, target):
        return pltpu.make_async_remote_copy(
            src_ref=src,
            dst_ref=dst,
            send_sem=send,
            recv_sem=recv,
            device_id=(group, target),
            device_id_type=MESH,
        )

    weights = [
        pltpu.make_async_copy(src, dst, w_sem.at[i])
        for i, (src, dst) in enumerate(
            ((wq_hbm, wq), (wk_hbm, wk), (wv_hbm, wv), (wo_hbm, wo))
        )
    ]
    for copy in weights:
        copy.start()

    barrier = pltpu.get_barrier_semaphore()

    @pl.loop(1, shards)
    def _(step):
        peer = lax.rem(me + step, shards)
        pl.semaphore_signal(barrier, inc=1, device_id=(group, peer), device_id_type=MESH)

    own_col = owner_ref[...]
    diag = iota((tokens, tokens), 0) == iota((tokens, tokens), 1)
    before = iota((tokens, tokens), 0) < iota((tokens, tokens), 1)
    own_row = jnp.sum(jnp.where(diag, own_col, 0), axis=0, keepdims=True)
    same = jnp.logical_and(own_col == own_row, before)
    rank_row = jnp.sum(jnp.where(same, 1, 0), axis=0, keepdims=True)
    place_row = own_row * padded + rank_row
    chosen = iota((places, tokens), 0) == place_row
    size_row = sizes_ref[...].astype(jnp.float32)
    size_col = jnp.sum(jnp.where(chosen, size_row, 0.0), axis=1, keepdims=True)
    size_tile = jnp.where(iota((places, LANES), 1) == 0, size_col, 0.0).astype(jnp.bfloat16)
    bucketed = jnp.dot(
        chosen.astype(jnp.float32).astype(jnp.bfloat16),
        tok_ref[...],
        preferred_element_type=jnp.float32,
    ).astype(jnp.bfloat16)
    for o in range(shards):
        rows = slice(o * padded, o * padded + slots)
        outgoing[o, :, 0:width] = bucketed[rows]
        outgoing[o, :, width : width + LANES] = size_tile[rows]

    pl.semaphore_wait(barrier, shards - 1)

    @pl.loop(1, shards)
    def _(step):
        peer = lax.rem(me + step, shards)
        remote(
            slot_ref.at[0], slots_in.at[me], slot_send.at[peer], slot_recv.at[me], peer
        ).start()
        remote(
            outgoing.at[peer], incoming.at[me], tok_send.at[peer], tok_recv.at[me], peer
        ).start()

    slots_in[me] = slot_ref[0]
    incoming[me] = outgoing[me]
    landed[...] = jnp.zeros_like(landed)
    wo_pad[...] = jnp.zeros_like(wo_pad)
    weights[3].wait()
    lead = 3 * HEAD - HEAD - LANES
    for h in range(HEADS):
        wo_pad[h, lead : lead + HEAD, :] = wo[h]

    @pl.loop(1, shards)
    def _(step):
        peer = lax.rem(me + step, shards)
        remote(
            slot_ref.at[0], slots_in.at[peer], slot_send.at[peer], slot_recv.at[peer], peer
        ).wait()

    tables = slots_in[...]
    table = jnp.sum(jnp.where(iota(tables.shape, 1) == me, tables, 0), axis=1)
    found = jnp.zeros((shards, tokens), jnp.int32)
    for r in range(slots):
        found = found + jnp.where(rank_row == r, table[:, r : r + 1], 0)
    found = jnp.where(iota((shards, tokens), 0) == own_row, found, 0)
    dest_row = own_row * merged_rows + jnp.sum(found, axis=0, keepdims=True)
    dest_out[:, 0:tokens] = jnp.broadcast_to(dest_row, (dest_out.shape[0], tokens))
    if tokens < dest_out.shape[1]:
        rest = dest_out.shape[1] - tokens
        dest_out[:, tokens:] = jnp.zeros((dest_out.shape[0], rest), jnp.int32)

    @pl.loop(1, HEADS)
    def _(step):
        head = lax.rem(my_head + step, HEADS)
        remote(
            dest_out, dest_in.at[my_head], dest_send.at[head], dest_recv.at[my_head],
            head * reps + my_rep,
        ).start()

    dest_in[my_head] = dest_out[...]

    own_table = slot_ref[0]
    lane = iota((shards, places), 1)
    target = jnp.zeros((shards, places), jnp.int32)
    for r in range(slots):
        target = target + jnp.where(lax.rem(lane, padded) == r, own_table[:, r : r + 1], 0)
    target = jnp.where(lane // padded == iota((shards, places), 0), target, 0)
    target_row = jnp.sum(target, axis=0, keepdims=True)
    landing = iota((merged_rows, places), 0) == target_row

    @pl.loop(1, shards)
    def _(step):
        peer = lax.rem(me + shards - step, shards)
        remote(
            outgoing.at[peer], incoming.at[peer], tok_send.at[peer], tok_recv.at[peer], peer
        ).wait()

    for e in range(shards):
        landed[e * padded : e * padded + slots, :] = incoming[e]
    pick = jnp.where(iota((8, LANES), 1) == 0, 1.0, 0.0).astype(jnp.bfloat16)
    weight_row = lax.dot_general(
        pick,
        landed[:, width : width + LANES],
        (((1,), (1,)), ((), ())),
        preferred_element_type=jnp.float32,
    )[0:1]
    weighted = jnp.where(landing, weight_row, 0.0)
    counts = jnp.sum(weighted, axis=1, keepdims=True)
    merged_sum = jnp.dot(
        weighted.astype(jnp.bfloat16), landed[:, 0:width], preferred_element_type=jnp.float32
    )
    merged = (merged_sum / jnp.maximum(counts, 1.0)).astype(jnp.bfloat16)
    bias = jnp.where(counts > 0, jnp.log(jnp.maximum(counts, 1.0)), -1e30)
    for copy in weights[:3]:
        copy.wait()
    spare = -model % LANES
    zeros = jnp.zeros((merged_rows, spare), jnp.float32)
    projected = [
        jnp.concatenate(
            [jnp.dot(merged, w[...], preferred_element_type=jnp.float32), zeros], axis=1
        )
        for w in (wq, wk, wv)
    ]
    lane = iota((merged_rows, pack), 1)
    for h in range(HEADS):
        block = jnp.where(lane == 3 * HEAD, bias, 0.0)
        first = h * HEAD // LANES * LANES
        for part in (2, 1, 0):
            window = projected[part][:, first : first + pack]
            shift = (part * HEAD - (h * HEAD - first)) % pack
            turned = pltpu.roll(window, shift, 1) if shift else window
            inside = jnp.logical_and(lane >= part * HEAD, lane < (part + 1) * HEAD)
            block = jnp.where(inside, turned, block)
        heads_out[h] = block.astype(jnp.bfloat16)

    @pl.loop(1, HEADS)
    def _(step):
        head = lax.rem(my_head + step, HEADS)
        remote(
            heads_out.at[head], heads_in.at[me], head_send.at[head], head_recv.at[me],
            head * reps + my_rep,
        ).start()

    heads_in[me] = heads_out[my_head]

    def share(step, source):
        partner = my_head * reps + lax.rem(my_rep + step, reps)
        return remote(
            heads_in.at[source],
            heads_in.at[source],
            share_send.at[step * shards + source],
            head_recv.at[source],
            partner,
        )

    @pl.loop(1, reps)
    def _(step):
        partner = my_head * reps + lax.rem(my_rep + step, reps)
        remote(
            heads_out.at[my_head],
            heads_in.at[me],
            share_send.at[step * shards + me],
            head_recv.at[me],
            partner,
        ).start()

    @pl.loop(1, HEADS)
    def _(step):
        source = lax.rem(my_head + HEADS - step, HEADS) * reps + my_rep
        remote(
            heads_out.at[my_head], heads_in.at[source], head_send.at[my_head],
            head_recv.at[source], source,
        ).wait_recv()

        @pl.loop(1, reps)
        def _(turn):
            share(turn, source).start()

    @pl.loop(1, HEADS)
    def _(step):
        other = lax.rem(my_head + HEADS - step, HEADS)
        remote(
            dest_out, dest_in.at[other], dest_send.at[other], dest_recv.at[other],
            other * reps + my_rep,
        ).wait()

    @pl.loop(1, reps)
    def _(step):
        rep = lax.rem(my_rep + reps - step, reps)

        @pl.loop(0, HEADS)
        def _(turn):
            source = lax.rem(my_head + HEADS - turn, HEADS) * reps + rep
            remote(
                heads_out.at[my_head], heads_in.at[source], head_send.at[my_head],
                head_recv.at[source], my_head * reps + rep,
            ).wait_recv()

    every = heads_in[...].reshape(total_rows, pack)
    pick = jnp.where(iota((8, pack), 1) == 3 * HEAD, 1.0, 0.0).astype(jnp.bfloat16)
    bias_row = lax.dot_general(
        pick, every, (((1,), (1,)), ((), ())), preferred_element_type=jnp.float32
    )[0:1]
    inverse = 1.0 / math.sqrt(HEAD)
    batch = HEADS // 2

    for turn in range(2):
        cols = []
        for b in range(batch):
            j = lax.rem(my_head + 1 + turn * batch + b, HEADS)
            row = dest_in[j][0:1, 0:tokens]
            cols.append(jnp.sum(jnp.where(diag, row, 0), axis=1, keepdims=True))
        column = jnp.concatenate(cols, axis=0)
        chosen = iota((batch * tokens, total_rows), 1) == column
        asked = jnp.dot(
            chosen.astype(jnp.float32).astype(jnp.bfloat16),
            every,
            preferred_element_type=jnp.float32,
        )
        asked = pltpu.roll(asked, HEAD, 1)
        lane = iota(asked.shape, 1)
        inside = jnp.logical_and(lane >= HEAD, lane < 2 * HEAD)
        asked = jnp.where(inside, asked, 0.0).astype(jnp.bfloat16)
        scores = lax.dot_general(
            asked, every, (((1,), (1,)), ((), ())), preferred_element_type=jnp.float32
        )
        scores = scores * inverse + bias_row
        expo = jnp.exp(scores - jnp.max(scores, axis=1, keepdims=True))
        total = jnp.sum(expo, axis=1, keepdims=True)
        accum = jnp.dot(
            expo.astype(jnp.bfloat16), every[:, LANES:], preferred_element_type=jnp.float32
        )
        attended = (accum / total).astype(jnp.bfloat16)
        for b in range(batch):
            j = lax.rem(my_head + 1 + turn * batch + b, HEADS)
            piece = attended[b * tokens : (b + 1) * tokens]
            if turn == 1 and b == batch - 1:
                att_in[my_head] = piece
            else:
                att_out[j] = piece
                remote(
                    att_out.at[j], att_in.at[my_head], att_send.at[j], att_recv.at[my_head],
                    j * reps + my_rep,
                ).start()

    @pl.loop(1, HEADS)
    def _(step):
        head = lax.rem(my_head + step, HEADS)
        remote(
            heads_out.at[head], heads_in.at[me], head_send.at[head], head_recv.at[me],
            head * reps + my_rep,
        ).wait_send()

    @pl.loop(1, reps)
    def _(step):
        @pl.loop(0, HEADS)
        def _(turn):
            share(step, lax.rem(my_head + turn, HEADS) * reps + my_rep).wait_send()

    @pl.loop(1, HEADS)
    def _(step):
        other = lax.rem(my_head + HEADS - step, HEADS)
        remote(
            att_out.at[other], att_in.at[other], att_send.at[other], att_recv.at[other],
            other * reps + my_rep,
        ).wait()

    result = jnp.zeros((tokens, width), jnp.float32)
    for h in range(0, HEADS, 2):
        both = jnp.concatenate([att_in[h], att_in[h + 1]], axis=1)
        result = result + jnp.dot(
            both,
            wo_pad[h : h + 2].reshape(2 * LANES, width),
            preferred_element_type=jnp.float32,
        )
    out_ref[...] = result.astype(jnp.bfloat16)


def on_device(tokens, owner, slot_map, sizes, w_query, w_key, w_value, w_out):
    shards = lax.axis_size("ctx")
    rows, width = tokens.shape
    slots = slot_map.shape[2]
    padded = -(-slots // 16) * 16
    merged_rows = rows // 2
    model = w_query.shape[1]
    pack = 2 * LANES
    reps = shards // HEADS
    vmem = pl.BlockSpec(memory_space=pltpu.VMEM)
    hbm = pl.BlockSpec(memory_space=pl.ANY)
    bf16 = jnp.bfloat16
    dma = pltpu.SemaphoreType.DMA
    aligned = -(-rows // LANES) * LANES
    return pl.pallas_call(
        functools.partial(kernel, shards),
        out_shape=jax.ShapeDtypeStruct((rows, width), bf16),
        in_specs=[vmem] * 4 + [hbm] * 4,
        out_specs=vmem,
        scratch_shapes=[
            pltpu.VMEM((width, model), bf16),
            pltpu.VMEM((width, model), bf16),
            pltpu.VMEM((width, model), bf16),
            pltpu.VMEM((HEADS, HEAD, width), bf16),
            pltpu.VMEM((HEADS, LANES, width), bf16),
            pltpu.VMEM((shards, shards, slots), jnp.int32),
            pltpu.VMEM((shards, slots, width + LANES), bf16),
            pltpu.VMEM((shards, slots, width + LANES), bf16),
            pltpu.VMEM((shards * padded, width + LANES), bf16),
            pltpu.VMEM((8, aligned), jnp.int32),
            pltpu.VMEM((HEADS, 8, aligned), jnp.int32),
            pltpu.VMEM((HEADS, merged_rows, pack), bf16),
            pltpu.VMEM((shards, merged_rows, pack), bf16),
            pltpu.VMEM((HEADS, rows, LANES), bf16),
            pltpu.VMEM((HEADS, rows, LANES), bf16),
            dma((4,)),
            dma((shards,)),
            dma((shards,)),
            dma((shards,)),
            dma((shards,)),
            dma((HEADS,)),
            dma((HEADS,)),
            dma((HEADS,)),
            dma((shards,)),
            dma((reps * shards,)),
            dma((HEADS,)),
            dma((HEADS,)),
            dma((1,)),
        ],
        compiler_params=pltpu.CompilerParams(
            collective_id=0, has_side_effects=True, vmem_limit_bytes=60 * 1024 * 1024
        ),
        name="merged_attention",
    )(
        tokens,
        owner,
        slot_map,
        sizes.reshape(1, rows),
        w_query,
        w_key,
        w_value,
        w_out.reshape(HEADS, HEAD, width),
    )


def solution(mesh):
    in_specs = (
        P(("groups", "ctx"), None),
        P(("groups", "ctx"), None),
        P(("groups", "ctx"), None, None),
        P(("groups", "ctx")),
        P(),
        P(),
        P(),
        P(),
    )
    out_specs = P(("groups", "ctx"), None)
    return jax.shard_map(
        on_device, mesh=mesh, in_specs=in_specs, out_specs=out_specs, check_vma=False
    )
```
